32 devices in a mesh: seq: 8 (over z, x), chan: 4 (over y, core).
Axes of the slice: x: 2, y: 2, z: 4, core: 2. Of those that a mesh axis runs over, the one named last changes fastest.
Arguments:
- q_proj: bfloat16 [4096, 1024], P('seq', 'chan'), may hold values from -6 to 6
- k_proj: bfloat16 [4096, 1024], P('seq', 'chan'), may hold values from -6 to 6
- v_proj: bfloat16 [4096, 1024], P('seq', 'chan'), may hold values from -6 to 6
- short_taps: float32 [3, 7, 1024], P(None, None, 'chan'), may hold values from -2 to 2
- medium_taps: float32 [128, 1024], P(None, 'chan'), may hold values from -0.5 to 0.5
- long_taps: float32 [4096, 1024], P('seq', 'chan'), may hold values from -0.09375 to 0.09375
- grad_out: bfloat16 [4096, 1024], P('seq', 'chan'), may hold values from -6 to 6
- stretch_grads: bfloat16 [1024, 1024], P(('seq', 'chan')), may hold values from -6 to 6
- positions: int32 [1024], replicated, may hold values from 0 to 4095, as said below
Outputs:
- y_out: bfloat16 [4096, 1024], P('seq', 'chan')
- grad_q: bfloat16 [4096, 1024], P('seq', 'chan')
- grad_k: bfloat16 [4096, 1024], P('seq', 'chan')
- grad_v: bfloat16 [4096, 1024], P('seq', 'chan')
- grad_long: float32 [4096, 1024], P('seq', 'chan')
The draws below stay inside these ranges and needn't reach their ends.
Inputs may be any that keep to these rules, and one draw needn't show every extreme that they name: 1024 distinct byte positions in increasing order; position 0 and position 4095 are always among them.
All inputs are finite; a program needn't handle non-finite values.
Results may differ from the reference program's by a relative error of at most 0.001.
Values may be sent and summed in bfloat16 or wider, within the bound.
A program may use at most 128 MiB of HBM per device.

```python
import jax
import jax.numpy as jnp
from jax import lax

D = 1024
SHORT = 7
MED = 128
ROWS = 512
LEN = 4096
STRETCHES = 1024


def draw_positions(key, part):
    weight_key, score_key = jax.random.split(key)
    blocks = LEN // ROWS
    weights = jax.random.randint(weight_key, (blocks,), 1, 9)
    raw_scores = jax.random.randint(score_key, (LEN,), 0, 1024)
    places = jnp.arange(LEN, dtype=jnp.int32)
    scores = raw_scores * weights[places // ROWS] * LEN + places
    forced = (places == 0) | (places == LEN - 1)
    scores = jnp.where(forced, 2147483647 - places, scores)
    _, chosen = lax.top_k(scores, STRETCHES)
    return jnp.sort(chosen).astype(jnp.int32)


def level_of(key, dims, shards, low, largest):
    gain, own = 1.0, jax.random.fold_in(key, 6)
    for position, parts in shards:
        draws = jnp.exp(jax.random.uniform(jax.random.fold_in(own, position), (parts,), jnp.float32, low / len(shards), largest / len(shards)))
        gain = gain * jnp.repeat(draws, dims[position] // parts).reshape([-1 if axis == position else 1 for axis in range(len(dims))])
    return gain


def centred(own_key, shape, spread, reach, cuts=(), kind=jnp.bfloat16):
    result = spread * jax.random.normal(own_key, shape, jnp.float32)
    if cuts:
        result = result * level_of(own_key, shape, cuts, -0.22, 0.18)
    return jnp.clip(result, -reach, reach).astype(kind)


def setup_inputs(seed: int = 0) -> dict:
    arg_keys = jax.random.split(jax.random.key(seed), 10)
    q_proj = centred(arg_keys[0], (LEN, D), 1.0, 6.0, ((0, 8), (1, 4)))
    k_proj = centred(arg_keys[1], (LEN, D), 1.0, 6.0, ((0, 8), (1, 4)))
    v_proj = centred(arg_keys[2], (LEN, D), 1.0, 6.0, ((0, 8), (1, 4)))
    short_taps = centred(arg_keys[3], (3, SHORT, D), SHORT ** -0.5, 2.0, ((2, 4),), jnp.float32)
    medium_taps = centred(arg_keys[4], (MED, D), MED ** -0.5, 0.5, ((1, 4),), jnp.float32)
    long_taps = centred(arg_keys[5], (LEN, D), LEN ** -0.5, 0.09375, ((0, 8), (1, 4)), jnp.float32)
    grad_out = centred(arg_keys[6], (LEN, D), 1.0, 6.0, ((0, 8), (1, 4)))
    stretch_grads = centred(arg_keys[7], (STRETCHES, D), 1.0, 6.0, ((0, 32),))
    positions = draw_positions(jax.random.fold_in(arg_keys[9], 71), 0)
    return {"q_proj": q_proj, "k_proj": k_proj, "v_proj": v_proj, "short_taps": short_taps, "medium_taps": medium_taps, "long_taps": long_taps, "grad_out": grad_out, "stretch_grads": stretch_grads, "positions": positions}


def causal(signal, taps):
    count = taps.shape[0]
    length = signal.shape[0]
    padded = jnp.pad(signal, ((count - 1, 0), (0, 0)))
    total = jnp.zeros_like(signal)
    for shift_by in range(count):
        start = count - 1 - shift_by
        total = total + taps[shift_by][None, :] * padded[start:start + length]
    return total


def anticausal(signal, taps):
    count = taps.shape[0]
    length = signal.shape[0]
    padded = jnp.pad(signal, ((0, count - 1), (0, 0)))
    total = jnp.zeros_like(signal)
    for shift_by in range(count):
        total = total + taps[shift_by][None, :] * padded[shift_by:shift_by + length]
    return total


def one_block(operands, positions):
    q_proj, k_proj, v_proj, short_taps, medium_taps, long_taps, grad_out, stretch_grads = operands
    q_short = causal(q_proj.astype(jnp.float32), short_taps[0])
    k_short = causal(k_proj.astype(jnp.float32), short_taps[1])
    v_short = causal(v_proj.astype(jnp.float32), short_taps[2])
    middle = causal(v_short, medium_taps)
    inner = k_short * middle
    padded_len = 2 * LEN
    spec_inner = jnp.fft.rfft(inner, padded_len, axis=0)
    spec_long = jnp.fft.rfft(long_taps, padded_len, axis=0)
    long_out = jnp.fft.irfft(spec_inner * spec_long, padded_len, axis=0)[:LEN]
    y_out = (q_short * long_out).astype(jnp.bfloat16)
    placed = jnp.zeros(q_short.shape, q_short.dtype).at[positions].add(stretch_grads.astype(q_short.dtype))
    out_grad = grad_out.astype(jnp.float32) + placed
    long_cot = out_grad * q_short
    q_back = out_grad * long_out
    spec_cot = jnp.fft.rfft(long_cot, padded_len, axis=0)
    inner_grad = jnp.fft.irfft(jnp.conj(spec_long) * spec_cot, padded_len, axis=0)[:LEN]
    grad_long = jnp.fft.irfft(jnp.conj(spec_inner) * spec_cot, padded_len, axis=0)[:LEN] * (LEN ** -0.5)
    k_back = inner_grad * middle
    mid_back = inner_grad * k_short
    v_back = anticausal(mid_back, medium_taps)
    grad_q = anticausal(q_back, short_taps[0]).astype(jnp.bfloat16)
    grad_k = anticausal(k_back, short_taps[1]).astype(jnp.bfloat16)
    grad_v = anticausal(v_back, short_taps[2]).astype(jnp.bfloat16)
    return (y_out, grad_q, grad_k, grad_v, grad_long.astype(jnp.float32))


def split_cols(array, blocks, block_width):
    lead = array.shape[:-1]
    moved = array.reshape(lead + (blocks, block_width))
    return jnp.moveaxis(moved, -2, 0)


def join_cols(array):
    moved = jnp.moveaxis(array, 0, -2)
    return moved.reshape(moved.shape[:-2] + (moved.shape[-2] * moved.shape[-1],))


def reference(q_proj, k_proj, v_proj, short_taps, medium_taps, long_taps, grad_out, stretch_grads, positions):
    block_width = 128 if D % 128 == 0 else D
    blocks = D // block_width
    operands = tuple(split_cols(item, blocks, block_width) for item in (q_proj, k_proj, v_proj, short_taps, medium_taps, long_taps, grad_out, stretch_grads))
    results = lax.map(lambda group: one_block(group, positions), operands)
    return tuple(join_cols(item) for item in results)
```

```python
import functools
import math

import jax
import jax.numpy as jnp
import numpy as np
from jax import lax
from jax.experimental import pallas as pl
from jax.experimental.pallas import tpu as pltpu
from jax.sharding import PartitionSpec as P

SHORT = 7
MED = 128
LANES = 128
f32 = jnp.float32
bf16 = jnp.bfloat16


def fourier(rows):
    full = 2 * rows
    order = np.concatenate([np.arange(0, rows, 2), np.arange(1, rows, 2)])
    time = np.arange(rows)
    angle = ((time[:, None] * order[None, :]) % full) * (2.0 * math.pi / full)
    real, imag = np.cos(angle), -np.sin(angle)
    imag[:, 0] = 1.0 - 2.0 * (time % 2)
    table = jnp.asarray(np.concatenate([real, imag], 1), f32)
    return table


def halves(x):
    high = x.astype(bf16)
    return high, (x - high.astype(f32)).astype(bf16)


def product(left, right, dims):
    (lh, ll), (rh, rl) = left, right
    dot = functools.partial(
        lax.dot_general, dimension_numbers=(dims, ((), ())), preferred_element_type=f32
    )
    return dot(lh, rh) + (dot(lh, rl) + dot(ll, rh))


def pack_kernel(q_ref, k_ref, v_ref, g_ref, l_ref, out_ref):
    rows = q_ref.shape[0]
    for slot, ref in enumerate((q_ref, k_ref, v_ref, g_ref)):
        out_ref[:, slot * rows : (slot + 1) * rows] = ref[...].astype(f32).T.astype(bf16)
    high, low = halves(l_ref[...].T)
    out_ref[:, 4 * rows : 5 * rows] = high
    out_ref[:, 5 * rows : 6 * rows] = low


def unpack_kernel(in_ref, y_ref, gq_ref, gk_ref, gv_ref, gl_ref):
    rows = y_ref.shape[0]
    for slot, ref in enumerate((y_ref, gq_ref, gk_ref, gv_ref)):
        ref[...] = in_ref[:, slot * rows : (slot + 1) * rows].astype(f32).T.astype(bf16)
    total = in_ref[:, 4 * rows : 5 * rows].astype(f32) + in_ref[:, 5 * rows : 6 * rows].astype(f32)
    gl_ref[...] = total.T


def from_before(tail, width):
    lane = lax.broadcasted_iota(jnp.int32, tail.shape, 1)
    return jnp.where(lane >= width, pltpu.roll(tail, width, 1), 0.0)


def from_after(head, width):
    lanes = head.shape[1]
    lane = lax.broadcasted_iota(jnp.int32, head.shape, 1)
    return jnp.where(lane < lanes - width, pltpu.roll(head, lanes - width, 1), 0.0)


def put(ref, start, value):
    for h in range(value.shape[1] // LANES):
        ref[h, start : start + value.shape[0], :] = value[:, h * LANES : (h + 1) * LANES]


def get(ref, start, size):
    return jnp.concatenate([ref[h, start : start + size, :] for h in range(ref.shape[0])], 1)


def operator_kernel(
    scale,
    in_ref,
    s_ref,
    pos_ref,
    st_ref,
    mt_ref,
    fh_ref,
    fl_ref,
    out_ref,
    ext,
    wide,
    turned,
    qs,
    ks,
    mid,
    og,
    xs,
    ls,
    cs,
    us,
):
    lanes = in_ref.shape[0]
    rows = in_ref.shape[1] // 6
    tiles = lanes // LANES
    count, _, width, _ = xs.shape
    table = (fh_ref[...], fl_ref[...])

    def block(slot):
        return in_ref[:, slot * rows : (slot + 1) * rows]

    def short_causal(slot, which, out, start):
        value = block(slot).astype(f32).T
        put(ext, 8, value)
        put(ext, 0, from_before(value[rows - 8 :], width))
        for h in range(tiles):
            for r in range(0, rows, LANES):
                acc = jnp.zeros((LANES, LANES), f32)
                for j in range(SHORT):
                    tap = st_ref[h, which * 8 + j : which * 8 + j + 1, :]
                    acc = acc + tap * ext[h, r + 8 - j : r + 8 - j + LANES, :]
                out[h, start + r : start + r + LANES, :] = acc

    def short_anti(value, which, slot):
        put(ext, 0, value)
        put(ext, rows, from_after(value[:8], width))
        for h in range(tiles):
            for r in range(0, rows, LANES):
                acc = jnp.zeros((LANES, LANES), f32)
                for j in range(SHORT):
                    tap = st_ref[h, which * 8 + j : which * 8 + j + 1, :]
                    acc = acc + tap * ext[h, r + j : r + j + LANES, :]
                out_ref[
                    h * LANES : (h + 1) * LANES, slot * rows + r : slot * rows + r + LANES
                ] = acc.T.astype(bf16)

    def medium(out, back):
        size = rows + MED
        for s in range(8):
            for h in range(tiles):
                start = s if back else 8 - s
                turned[s, h, :, :] = wide[h, start : start + size, :]

        def step(n, carry):
            h = n // (rows // LANES)
            base = pl.multiple_of((n % (rows // LANES)) * LANES, LANES)
            acc = jnp.zeros((LANES, LANES), f32)
            for s in range(8):
                window = turned[s, h, pl.ds(base, LANES + MED), :]
                for m in range(MED // 8):
                    lead = 8 * m if back else MED - 8 * m
                    tap = mt_ref[h, 8 * m + s : 8 * m + s + 1, :]
                    acc = acc + tap * window[lead : lead + LANES]
            out[h, pl.ds(base, LANES), :] = acc
            return carry

        lax.fori_loop(0, tiles * (rows // LANES), step, 0)

    short_causal(0, 0, qs, 0)
    short_causal(1, 1, ks, 0)
    short_causal(2, 2, wide, MED + 8)
    put(wide, 8, from_before(get(wide, 8 + rows, MED), width))
    for h in range(tiles):
        wide[h, 0:8, :] = jnp.zeros((8, LANES), f32)
    medium(mid, False)

    stretches = pos_ref.shape[0]
    for a in range(count):
        spot = lax.broadcasted_iota(jnp.int32, (stretches, rows), 1) + a * rows
        onehot = (pos_ref[...] == spot).astype(f32).astype(bf16)
        placed = jnp.dot(s_ref[...], onehot, preferred_element_type=f32)
        piece = in_ref[a * width : (a + 1) * width, 3 * rows : 4 * rows].astype(f32) + placed
        us[a * width : (a + 1) * width, 0:rows] = piece
    put(og, 0, us[:, 0:rows].T)

    first = lax.broadcasted_iota(jnp.int32, (count, width, rows), 2) == 0

    def keep(ref, signal, masked):
        spectrum = product(signal, table, ((1,), (0,)))
        real = spectrum[:, :rows].reshape(count, width, rows)
        imag = spectrum[:, rows:].reshape(count, width, rows)
        ref[:, 0] = real
        ref[:, 1] = jnp.where(first, 0.0, imag) if masked else imag
        if masked:
            ref[:, 2] = jnp.where(first, imag, real)

    keep(ls, (block(4), block(5)), True)
    keep(xs, halves((get(ks, 0, rows) * get(mid, 0, rows)).T), True)
    keep(cs, halves((get(og, 0, rows) * get(qs, 0, rows)).T), False)

    lane = lax.broadcasted_iota(jnp.int32, (width, rows), 1)
    weight = jnp.where(lane == 0, 1.0, 2.0) / (2 * rows)
    sign = jnp.where(lane < rows // 2, 1.0, -1.0) * weight
    zero = jnp.zeros((width, rows), f32)

    def emit(i, now, before, factor):
        base = pl.multiple_of(i * width, width)
        us[pl.ds(base, width), 0:rows] = (now[0] * weight + before[0] * sign) * factor
        us[pl.ds(base, width), rows : 2 * rows] = (now[1] * weight + before[1] * sign) * factor

    def convolve():
        def outer(i, before):
            def inner(b, total):
                xr, lr, li, lq = xs[i - b, 0], ls[b, 0], ls[b, 1], ls[b, 2]
                masked = xs[i - b, 1]
                xi = jnp.where(lane == 0, xs[i - b, 2], masked)
                return (
                    total[0] + (xr * lr - xi * li),
                    total[1] + (xr * li + xi * lq),
                )

            now = lax.fori_loop(0, i + 1, inner, (zero, zero))
            emit(i, now, before, 1.0)
            return now

        lax.fori_loop(0, count, outer, (zero, zero))

    def correlate(ref, factor):
        def outer(n, before):
            d = count - 1 - n

            def inner(b, total):
                cr, ci = cs[b + d, 0], cs[b + d, 1]
                ar, ai, aq = ref[b, 0], ref[b, 1], ref[b, 2]
                return (
                    total[0] + (cr * ar + ci * ai),
                    total[1] + (ci * aq - cr * ai),
                )

            now = lax.fori_loop(0, n + 1, inner, (zero, zero))
            emit(d, now, before, factor)
            return now

        lax.fori_loop(0, count, outer, (zero, zero))

    correlate(xs, scale)
    high, low = halves(product(halves(us[...]), table, ((1,), (1,))))
    out_ref[:, 4 * rows : 5 * rows] = high
    out_ref[:, 5 * rows : 6 * rows] = low

    convolve()
    long_out = product(table, halves(us[...]), ((1,), (1,)))
    out_ref[:, 0:rows] = (get(qs, 0, rows) * long_out).T.astype(bf16)
    short_anti(get(og, 0, rows) * long_out, 0, 1)

    correlate(ls, 1.0)
    inner_grad = product(table, halves(us[...]), ((1,), (1,)))
    mid_back = inner_grad * get(ks, 0, rows)
    put(wide, 0, mid_back)
    put(wide, rows, from_after(mid_back[:MED], width))
    for h in range(tiles):
        wide[h, rows + MED : rows + MED + 8, :] = jnp.zeros((8, LANES), f32)
    short_anti(inner_grad * get(mid, 0, rows), 1, 2)
    medium(qs, True)
    short_anti(get(qs, 0, rows), 2, 3)


def whole_spec(n):
    return [pl.BlockSpec(memory_space=pltpu.VMEM)] * n


def local(
    q_proj, k_proj, v_proj, short_taps, medium_taps, long_taps, grad_out, stretch_grads, positions
):
    rows, lanes = q_proj.shape
    count = lax.axis_size("seq")
    index = lax.axis_index("seq")
    width = lanes // count
    tiles = lanes // LANES

    packed = pl.pallas_call(
        pack_kernel,
        out_shape=jax.ShapeDtypeStruct((lanes, 6 * rows), bf16),
        in_specs=whole_spec(5),
        out_specs=whole_spec(1)[0],
        name="pack",
    )(q_proj, k_proj, v_proj, grad_out, long_taps)

    mine = lax.all_to_all(stretch_grads, "chan", split_axis=1, concat_axis=0, tiled=True)
    mine = mine.T.reshape(count, width, mine.shape[0])
    stretch = lax.all_to_all(mine, "seq", split_axis=0, concat_axis=0, tiled=True)
    stretch = stretch.transpose(1, 0, 2).reshape(width, -1)

    arrived = lax.all_to_all(
        packed.reshape(count, width, 6 * rows), "seq", split_axis=0, concat_axis=0, tiled=True
    ).reshape(lanes, 6 * rows)

    def spread(taps):
        part = lax.dynamic_slice_in_dim(taps, index * width, width, 1)
        part = jnp.tile(part, (1, count))
        return part.reshape(taps.shape[0], tiles, LANES).transpose(1, 0, 2)

    short = spread(jnp.pad(short_taps, ((0, 0), (0, 1), (0, 0))).reshape(24, lanes))
    medium = spread(medium_taps)
    table = fourier(rows)
    fh, fl = halves(table)
    scratch = [
        pltpu.VMEM((tiles, rows + 8, LANES), f32),
        pltpu.VMEM((tiles, rows + MED + 8, LANES), f32),
        pltpu.VMEM((8, tiles, rows + MED, LANES), f32),
        pltpu.VMEM((tiles, rows, LANES), f32),
        pltpu.VMEM((tiles, rows, LANES), f32),
        pltpu.VMEM((tiles, rows, LANES), f32),
        pltpu.VMEM((tiles, rows, LANES), f32),
        pltpu.VMEM((count, 3, width, rows), f32),
        pltpu.VMEM((count, 3, width, rows), f32),
        pltpu.VMEM((count, 2, width, rows), f32),
        pltpu.VMEM((lanes, 2 * rows), f32),
    ]
    result = pl.pallas_call(
        functools.partial(operator_kernel, (rows * count) ** (-0.5)),
        out_shape=jax.ShapeDtypeStruct((lanes, 6 * rows), bf16),
        in_specs=whole_spec(7),
        out_specs=whole_spec(1)[0],
        scratch_shapes=scratch,
        name="operator",
    )(arrived, stretch, positions[:, None], short, medium, fh, fl)

    back = lax.all_to_all(
        result.reshape(count, width, 6 * rows), "seq", split_axis=0, concat_axis=0, tiled=True
    ).reshape(lanes, 6 * rows)
    return pl.pallas_call(
        unpack_kernel,
        out_shape=[jax.ShapeDtypeStruct((rows, lanes), bf16)] * 4
        + [jax.ShapeDtypeStruct((rows, lanes), f32)],
        in_specs=whole_spec(1),
        out_specs=whole_spec(5),
        name="unpack",
    )(back)


def solution(mesh):
    return jax.shard_map(
        local,
        mesh=mesh,
        in_specs=(
            P("seq", "chan"),
            P("seq", "chan"),
            P("seq", "chan"),
            P(None, None, "chan"),
            P(None, "chan"),
            P("seq", "chan"),
            P("seq", "chan"),
            P(("seq", "chan"), None),
            P(),
        ),
        out_specs=(
            P("seq", "chan"),
            P("seq", "chan"),
            P("seq", "chan"),
            P("seq", "chan"),
            P("seq", "chan"),
        ),
        check_vma=False,
    )
```

```python
import functools
import math

import jax
import jax.numpy as jnp
import numpy as np
from jax import lax
from jax.experimental import pallas as pl
from jax.experimental.pallas import tpu as pltpu
from jax.sharding import PartitionSpec as P

SHORT = 7
MED = 128
LANES = 128
f32 = jnp.float32
bf16 = jnp.bfloat16


def fourier(rows):
    full = 2 * rows
    order = np.concatenate([np.arange(0, rows, 2), np.arange(1, rows, 2)])
    time = np.arange(rows)
    angle = ((time[:, None] * order[None, :]) % full) * (2.0 * math.pi / full)
    real, imag = np.cos(angle), -np.sin(angle)
    imag[:, 0] = 1.0 - 2.0 * (time % 2)
    table = jnp.asarray(np.concatenate([real, imag], 1), f32)
    return table


def halves(x):
    high = x.astype(bf16)
    return high, (x - high.astype(f32)).astype(bf16)


def product(left, right, dims):
    (lh, ll), (rh, rl) = left, right
    dot = functools.partial(
        lax.dot_general, dimension_numbers=(dims, ((), ())), preferred_element_type=f32
    )
    return dot(lh, rh) + (dot(lh, rl) + dot(ll, rh))


def pack_kernel(q_ref, k_ref, v_ref, g_ref, s_ref, out_ref, landed, send_sem, recv_sem, own_sem):
    rows, lanes = q_ref.shape
    members = landed.shape[0]
    me = lax.axis_index("chan")

    def columns(who):
        return s_ref.at[:, pl.ds(pl.multiple_of(who * lanes, lanes), lanes)]

    own = pltpu.make_async_copy(columns(me), landed.at[me], own_sem)
    own.start()
    copies = []
    if members > 1:
        barrier = pltpu.get_barrier_semaphore()
        for step in range(1, members):
            peer = lax.rem(me + step, members)
            pl.semaphore_signal(
                barrier, inc=1, device_id={"chan": peer}, device_id_type=pl.DeviceIdType.MESH
            )
        pl.semaphore_wait(barrier, members - 1)
        for step in range(1, members):
            peer = lax.rem(me + step, members)
            copy = pltpu.make_async_remote_copy(
                src_ref=columns(peer),
                dst_ref=landed.at[me],
                send_sem=send_sem.at[step],
                recv_sem=recv_sem.at[step],
                device_id={"chan": peer},
                device_id_type=pl.DeviceIdType.MESH,
            )
            copy.start()
            copies.append(copy)
    for slot, ref in enumerate((q_ref, k_ref, v_ref, g_ref)):
        out_ref[:, slot * rows : (slot + 1) * rows] = ref[...].astype(f32).T.astype(bf16)
    own.wait()
    for copy in copies:
        copy.wait()
    stretch = jnp.concatenate([landed[j].astype(f32) for j in range(members)], 0)
    out_ref[:, 4 * rows :] = stretch.T.astype(bf16)


def pack_long_kernel(l_ref, out_ref):
    rows = l_ref.shape[0]
    high, low = halves(l_ref[...].T)
    out_ref[:, :rows] = high
    out_ref[:, rows:] = low


def unpack_kernel(in_ref, a_ref, b_ref):
    rows = a_ref.shape[0]
    a_ref[...] = in_ref[:, :rows].astype(f32).T.astype(bf16)
    b_ref[...] = in_ref[:, rows:].astype(f32).T.astype(bf16)


def unpack_long_kernel(in_ref, gl_ref):
    rows = gl_ref.shape[0]
    gl_ref[...] = (in_ref[:, :rows].astype(f32) + in_ref[:, rows:].astype(f32)).T


def from_before(tail, width):
    lane = lax.broadcasted_iota(jnp.int32, tail.shape, 1)
    return jnp.where(lane >= width, pltpu.roll(tail, width, 1), 0.0)


def from_after(head, width):
    lanes = head.shape[1]
    lane = lax.broadcasted_iota(jnp.int32, head.shape, 1)
    return jnp.where(lane < lanes - width, pltpu.roll(head, lanes - width, 1), 0.0)


def put(ref, start, value):
    for h in range(value.shape[1] // LANES):
        ref[h, start : start + value.shape[0], :] = value[:, h * LANES : (h + 1) * LANES]


def get(ref, start, size):
    return jnp.concatenate([ref[h, start : start + size, :] for h in range(ref.shape[0])], 1)


def taps_sum(src, taps, which, h, r, back):
    acc = jnp.zeros((LANES, LANES), f32)
    for j in range(SHORT):
        tap = taps[h, which * 8 + j : which * 8 + j + 1, :]
        lead = j if back else 8 - j
        acc = acc + tap * src[h, r + lead : r + lead + LANES, :]
    return acc


def short_causal(value, which, ext, taps, width, out, start):
    rows = value.shape[0]
    put(ext, 8, value)
    put(ext, 0, from_before(value[rows - 8 :], width))
    for h in range(ext.shape[0]):
        for r in range(0, rows, LANES):
            out[h, start + r : start + r + LANES, :] = taps_sum(ext, taps, which, h, r, False)


def short_anti(value, which, ext, taps, width, out, slot):
    rows = value.shape[0]
    put(ext, 0, value)
    put(ext, rows, from_after(value[:8], width))
    for h in range(ext.shape[0]):
        for r in range(0, rows, LANES):
            out[h * LANES : (h + 1) * LANES, slot * rows + r : slot * rows + r + LANES] = (
                taps_sum(ext, taps, which, h, r, True).T.astype(bf16)
            )


def medium(wide, turned, taps, out, back):
    tiles, size, _ = turned.shape[1:]
    steps = (size - MED) // LANES
    for s in range(8):
        for h in range(tiles):
            start = s if back else 8 - s
            turned[s, h, :, :] = wide[h, start : start + size, :]

    def step(n, carry):
        h = n // steps
        base = pl.multiple_of((n % steps) * LANES, LANES)
        acc = jnp.zeros((LANES, LANES), f32)
        for s in range(8):
            window = turned[s, h, pl.ds(base, LANES + MED), :]
            for m in range(MED // 8):
                lead = 8 * m if back else MED - 8 * m
                tap = taps[h, 8 * m + s : 8 * m + s + 1, :]
                acc = acc + tap * window[lead : lead + LANES]
        out[h, pl.ds(base, LANES), :] = acc
        return carry

    lax.fori_loop(0, tiles * steps, step, 0)


def keep(ref, signal, table, masked):
    count, _, width, rows = ref.shape
    spectrum = product(signal, table, ((1,), (0,)))
    real = spectrum[:, :rows].reshape(count, width, rows)
    imag = spectrum[:, rows:].reshape(count, width, rows)
    ref[:, 0] = real
    if not masked:
        ref[:, 1] = imag
        return
    first = lax.broadcasted_iota(jnp.int32, (count, width, rows), 2) == 0
    ref[:, 1] = jnp.where(first, 0.0, imag)
    ref[:, 2] = jnp.where(first, imag, real)


def emitter(us, width, rows, factor):
    lane = lax.broadcasted_iota(jnp.int32, (width, rows), 1)
    weight = jnp.where(lane == 0, 1.0, 2.0) * (factor / (2 * rows))
    sign = jnp.where(lane < rows // 2, 1.0, -1.0) * weight

    def emit(i, now, before):
        base = pl.multiple_of(i * width, width)
        us[pl.ds(base, width), 0:rows] = now[0] * weight + before[0] * sign
        us[pl.ds(base, width), rows : 2 * rows] = now[1] * weight + before[1] * sign

    return emit


def convolve(xs, ls, us):
    count, _, width, rows = xs.shape
    emit = emitter(us, width, rows, 1.0)
    zero = jnp.zeros((width, rows), f32)
    lane = lax.broadcasted_iota(jnp.int32, (width, rows), 1)

    def outer(i, before):
        def inner(b, total):
            xr, lr, li, lq = xs[i - b, 0], ls[b, 0], ls[b, 1], ls[b, 2]
            xi = jnp.where(lane == 0, xs[i - b, 2], xs[i - b, 1])
            return (total[0] + (xr * lr - xi * li), total[1] + (xr * li + xi * lq))

        now = lax.fori_loop(0, i + 1, inner, (zero, zero))
        emit(i, now, before)
        return now

    lax.fori_loop(0, count, outer, (zero, zero))


def correlate(ref, cs, us, factor):
    count, _, width, rows = ref.shape
    emit = emitter(us, width, rows, factor)
    zero = jnp.zeros((width, rows), f32)

    def outer(n, before):
        d = count - 1 - n

        def inner(b, total):
            cr, ci = cs[b + d, 0], cs[b + d, 1]
            ar, ai, aq = ref[b, 0], ref[b, 1], ref[b, 2]
            return (total[0] + (cr * ar + ci * ai), total[1] + (ci * aq - cr * ai))

        now = lax.fori_loop(0, n + 1, inner, (zero, zero))
        emit(d, now, before)
        return now

    lax.fori_loop(0, count, outer, (zero, zero))


def gates_kernel(
    scale, in_ref, pos_ref, st_ref, mt_ref, fh_ref, fl_ref,
    gl_ref, qs, ks, mid, og, xs, cs,
    ext, wide, turned, us,
):
    tiles = ext.shape[0]
    count, _, width, rows = xs.shape
    table = (fh_ref[...], fl_ref[...])

    def block(slot):
        return in_ref[:, slot * rows : (slot + 1) * rows].astype(f32).T

    short_causal(block(0), 0, ext, st_ref, width, qs, 0)
    short_causal(block(1), 1, ext, st_ref, width, ks, 0)
    short_causal(block(2), 2, ext, st_ref, width, wide, MED + 8)
    put(wide, 8, from_before(get(wide, 8 + rows, MED), width))
    for h in range(tiles):
        wide[h, 0:8, :] = jnp.zeros((8, LANES), f32)
    medium(wide, turned, mt_ref, mid, False)

    stretches = pos_ref.shape[0]
    stretch = jnp.concatenate(
        [in_ref[b * width : (b + 1) * width, 4 * rows :] for b in range(count)], 1
    )
    for a in range(count):
        spot = lax.broadcasted_iota(jnp.int32, (stretches, rows), 1) + a * rows
        onehot = (pos_ref[...] == spot).astype(f32).astype(bf16)
        placed = jnp.dot(stretch, onehot, preferred_element_type=f32)
        piece = in_ref[a * width : (a + 1) * width, 3 * rows : 4 * rows].astype(f32) + placed
        us[a * width : (a + 1) * width, 0:rows] = piece
    put(og, 0, us[:, 0:rows].T)

    keep(xs, halves((get(ks, 0, rows) * get(mid, 0, rows)).T), table, True)
    keep(cs, halves((get(og, 0, rows) * get(qs, 0, rows)).T), table, False)
    correlate(xs, cs, us, scale)
    high, low = halves(product(halves(us[...]), table, ((1,), (1,))))
    gl_ref[:, :rows] = high
    gl_ref[:, rows:] = low


def output_kernel(l_ref, xs, qs, og, st_ref, fh_ref, fl_ref, out_ref, ls, ext, us):
    _, _, width, rows = xs.shape
    table = (fh_ref[...], fl_ref[...])
    keep(ls, (l_ref[:, :rows], l_ref[:, rows:]), table, True)
    convolve(xs, ls, us)
    long_out = product(table, halves(us[...]), ((1,), (1,)))
    out_ref[:, 0:rows] = (get(qs, 0, rows) * long_out).T.astype(bf16)
    short_anti(get(og, 0, rows) * long_out, 0, ext, st_ref, width, out_ref, 1)


def back_kernel(ls, cs, ks, mid, st_ref, mt_ref, fh_ref, fl_ref, out_ref, ext, wide, turned, us, vb):
    _, _, width, rows = ls.shape
    table = (fh_ref[...], fl_ref[...])
    correlate(ls, cs, us, 1.0)
    inner_grad = product(table, halves(us[...]), ((1,), (1,)))
    mid_back = inner_grad * get(ks, 0, rows)
    put(wide, 0, mid_back)
    put(wide, rows, from_after(mid_back[:MED], width))
    for h in range(ext.shape[0]):
        wide[h, rows + MED : rows + MED + 8, :] = jnp.zeros((8, LANES), f32)
    short_anti(inner_grad * get(mid, 0, rows), 1, ext, st_ref, width, out_ref, 0)
    medium(wide, turned, mt_ref, vb, True)
    short_anti(get(vb, 0, rows), 2, ext, st_ref, width, out_ref, 1)


def whole_spec(n):
    return [pl.BlockSpec(memory_space=pltpu.VMEM)] * n


def local(
    q_proj, k_proj, v_proj, short_taps, medium_taps, long_taps, grad_out, stretch_grads, positions
):
    rows, lanes = q_proj.shape
    count = lax.axis_size("seq")
    index = lax.axis_index("seq")
    width = lanes // count
    tiles = lanes // LANES

    shape = jax.ShapeDtypeStruct

    def call(kernel, outs, args, scratch=(), micros=3):
        many = len(outs) > 1
        return pl.pallas_call(
            kernel,
            out_shape=outs if many else outs[0],
            in_specs=whole_spec(len(args)),
            out_specs=whole_spec(len(outs)) if many else whole_spec(1)[0],
            scratch_shapes=list(scratch),
            cost_estimate=pl.CostEstimate(
                flops=micros * 10**9, bytes_accessed=micros * 3 * 10**6, transcendentals=0
            ),
        )(*args)

    def regroup(array):
        split = array.reshape(count, width, array.shape[1])
        moved = lax.all_to_all(split, "seq", split_axis=0, concat_axis=0, tiled=True)
        return moved.reshape(array.shape)

    pair = shape((lanes, 2 * rows), bf16)
    signal = shape((tiles, rows, LANES), f32)
    three = shape((count, 3, width, rows), f32)
    two = shape((count, 2, width, rows), f32)
    ext = pltpu.VMEM((tiles, rows + 8, LANES), f32)
    wide = pltpu.VMEM((tiles, rows + MED + 8, LANES), f32)
    turned = pltpu.VMEM((8, tiles, rows + MED, LANES), f32)
    spectrum = pltpu.VMEM((lanes, 2 * rows), f32)

    members = lax.axis_size("chan")
    stretches = stretch_grads.shape[0]
    packed = pl.pallas_call(
        pack_kernel,
        out_shape=shape((lanes, 4 * rows + members * stretches), bf16),
        in_specs=whole_spec(5),
        out_specs=whole_spec(1)[0],
        scratch_shapes=[
            pltpu.VMEM((members, stretches, lanes), bf16),
            pltpu.SemaphoreType.DMA((members,)),
            pltpu.SemaphoreType.DMA((members,)),
            pltpu.SemaphoreType.DMA,
        ],
        compiler_params=pltpu.CompilerParams(
            collective_id=0 if members > 1 else None, has_side_effects=True
        ),
        name="pack",
    )(q_proj, k_proj, v_proj, grad_out, stretch_grads)
    arrived = regroup(packed)
    long_packed = call(pack_long_kernel, [pair], (long_taps,))
    long_arrived = regroup(long_packed)

    def spread(taps):
        part = lax.dynamic_slice_in_dim(taps, index * width, width, 1)
        part = jnp.tile(part, (1, count))
        return part.reshape(taps.shape[0], tiles, LANES).transpose(1, 0, 2)

    short = spread(jnp.pad(short_taps, ((0, 0), (0, 1), (0, 0))).reshape(24, lanes))
    medium_part = spread(medium_taps)
    fh, fl = halves(fourier(rows))
    gl, qs, ks, mid, og, xs, cs = call(
        functools.partial(gates_kernel, (rows * count) ** (-0.5)),
        [pair, signal, signal, signal, signal, three, two],
        (arrived, positions[:, None], short, medium_part, fh, fl),
        (ext, wide, turned, spectrum),
        20,
    )
    gl_back = regroup(gl)
    y_gq, ls = call(
        output_kernel, [pair, three], (long_arrived, xs, qs, og, short, fh, fl), (ext, spectrum), 8
    )
    y_back = regroup(y_gq)
    gk_gv = call(
        back_kernel,
        [pair],
        (ls, cs, ks, mid, short, medium_part, fh, fl),
        (ext, wide, turned, spectrum, pltpu.VMEM((tiles, rows, LANES), f32)),
        12,
    )
    k_back = regroup(gk_gv)
    half = shape((rows, lanes), bf16)
    grad_long = call(unpack_long_kernel, [shape((rows, lanes), f32)], (gl_back,))
    y_out, grad_q = call(unpack_kernel, [half, half], (y_back,))
    grad_k, grad_v = call(unpack_kernel, [half, half], (k_back,))
    return (y_out, grad_q, grad_k, grad_v, grad_long)


def solution(mesh):
    return jax.shard_map(
        local,
        mesh=mesh,
        in_specs=(
            P("seq", "chan"),
            P("seq", "chan"),
            P("seq", "chan"),
            P(None, None, "chan"),
            P(None, "chan"),
            P("seq", "chan"),
            P("seq", "chan"),
            P(("seq", "chan"), None),
            P(),
        ),
        out_specs=(
            P("seq", "chan"),
            P("seq", "chan"),
            P("seq", "chan"),
            P("seq", "chan"),
            P("seq", "chan"),
        ),
        check_vma=False,
    )
```

```python
import functools
import math

import jax
import jax.numpy as jnp
import numpy as np
from jax import lax
from jax.experimental import pallas as pl
from jax.experimental.pallas import tpu as pltpu
from jax.sharding import PartitionSpec as P

SHORT = 7
MED = 128
LANES = 128
f32 = jnp.float32
bf16 = jnp.bfloat16


def fourier(rows):
    full = 2 * rows
    order = np.concatenate([np.arange(0, rows, 2), np.arange(1, rows, 2)])
    time = np.arange(rows)
    angle = ((time[:, None] * order[None, :]) % full) * (2.0 * math.pi / full)
    real, imag = np.cos(angle), -np.sin(angle)
    imag[:, 0] = 1.0 - 2.0 * (time % 2)
    table = jnp.asarray(np.concatenate([real, imag], 1), f32)
    return table


def halves(x):
    high = x.astype(bf16)
    return high, (x - high.astype(f32)).astype(bf16)


def product(left, right, dims):
    (lh, ll), (rh, rl) = left, right
    dot = functools.partial(
        lax.dot_general, dimension_numbers=(dims, ((), ())), preferred_element_type=f32
    )
    return dot(lh, rh) + (dot(lh, rl) + dot(ll, rh))


def pack_kernel(q_ref, g_ref, l_ref, s_ref, out_ref, landed, send_sem, recv_sem, own_sem):
    rows, lanes = q_ref.shape
    members = landed.shape[0]
    me = lax.axis_index("chan")

    def columns(who):
        return s_ref.at[:, pl.ds(pl.multiple_of(who * lanes, lanes), lanes)]

    own = pltpu.make_async_copy(columns(me), landed.at[me], own_sem)
    own.start()
    copies = []
    if members > 1:
        barrier = pltpu.get_barrier_semaphore()
        for step in range(1, members):
            peer = lax.rem(me + step, members)
            pl.semaphore_signal(
                barrier, inc=1, device_id={"chan": peer}, device_id_type=pl.DeviceIdType.MESH
            )
        pl.semaphore_wait(barrier, members - 1)
        for step in range(1, members):
            peer = lax.rem(me + step, members)
            copy = pltpu.make_async_remote_copy(
                src_ref=columns(peer),
                dst_ref=landed.at[me],
                send_sem=send_sem.at[step],
                recv_sem=recv_sem.at[step],
                device_id={"chan": peer},
                device_id_type=pl.DeviceIdType.MESH,
            )
            copy.start()
            copies.append(copy)
    for slot, ref in enumerate((q_ref, g_ref)):
        out_ref[:, slot * rows : (slot + 1) * rows] = ref[...].astype(f32).T.astype(bf16)
    high, low = halves(l_ref[...].T)
    out_ref[:, 2 * rows : 3 * rows] = high
    out_ref[:, 3 * rows : 4 * rows] = low
    own.wait()
    for copy in copies:
        copy.wait()
    stretch = jnp.concatenate([landed[j].astype(f32) for j in range(members)], 0)
    out_ref[:, 4 * rows :] = stretch.T.astype(bf16)


def pack_first_kernel(k_ref, v_ref, out_ref):
    rows = k_ref.shape[0]
    out_ref[:, :rows] = k_ref[...].astype(f32).T.astype(bf16)
    out_ref[:, rows:] = v_ref[...].astype(f32).T.astype(bf16)


def unpack_kernel(in_ref, a_ref, b_ref):
    rows = a_ref.shape[0]
    a_ref[...] = in_ref[:, :rows].astype(f32).T.astype(bf16)
    b_ref[...] = in_ref[:, rows:].astype(f32).T.astype(bf16)


def unpack_long_kernel(in_ref, gl_ref):
    rows = gl_ref.shape[0]
    gl_ref[...] = (in_ref[:, :rows].astype(f32) + in_ref[:, rows:].astype(f32)).T


def from_before(tail, width):
    lane = lax.broadcasted_iota(jnp.int32, tail.shape, 1)
    return jnp.where(lane >= width, pltpu.roll(tail, width, 1), 0.0)


def from_after(head, width):
    lanes = head.shape[1]
    lane = lax.broadcasted_iota(jnp.int32, head.shape, 1)
    return jnp.where(lane < lanes - width, pltpu.roll(head, lanes - width, 1), 0.0)


def put(ref, start, value):
    for h in range(value.shape[1] // LANES):
        ref[h, start : start + value.shape[0], :] = value[:, h * LANES : (h + 1) * LANES]


def get(ref, start, size):
    return jnp.concatenate([ref[h, start : start + size, :] for h in range(ref.shape[0])], 1)


def taps_sum(src, taps, which, h, r, back):
    acc = jnp.zeros((LANES, LANES), f32)
    for j in range(SHORT):
        tap = taps[h, which * 8 + j : which * 8 + j + 1, :]
        lead = j if back else 8 - j
        acc = acc + tap * src[h, r + lead : r + lead + LANES, :]
    return acc


def short_causal(value, which, ext, taps, width, out, start):
    rows = value.shape[0]
    put(ext, 8, value)
    put(ext, 0, from_before(value[rows - 8 :], width))
    for h in range(ext.shape[0]):
        for r in range(0, rows, LANES):
            out[h, start + r : start + r + LANES, :] = taps_sum(ext, taps, which, h, r, False)


def short_anti(value, which, ext, taps, width, out, slot):
    rows = value.shape[0]
    put(ext, 0, value)
    put(ext, rows, from_after(value[:8], width))
    for h in range(ext.shape[0]):
        for r in range(0, rows, LANES):
            out[h * LANES : (h + 1) * LANES, slot * rows + r : slot * rows + r + LANES] = (
                taps_sum(ext, taps, which, h, r, True).T.astype(bf16)
            )


def medium(wide, turned, taps, out, back):
    tiles, size, _ = turned.shape[1:]
    steps = (size - MED) // LANES
    for s in range(8):
        for h in range(tiles):
            start = s if back else 8 - s
            turned[s, h, :, :] = wide[h, start : start + size, :]

    def step(n, carry):
        h = n // steps
        base = pl.multiple_of((n % steps) * LANES, LANES)
        acc = jnp.zeros((LANES, LANES), f32)
        for s in range(8):
            window = turned[s, h, pl.ds(base, LANES + MED), :]
            for m in range(MED // 8):
                lead = 8 * m if back else MED - 8 * m
                tap = taps[h, 8 * m + s : 8 * m + s + 1, :]
                acc = acc + tap * window[lead : lead + LANES]
        out[h, pl.ds(base, LANES), :] = acc
        return carry

    lax.fori_loop(0, tiles * steps, step, 0)


def keep(ref, signal, table, masked):
    count, _, width, rows = ref.shape
    spectrum = product(signal, table, ((1,), (0,)))
    real = spectrum[:, :rows].reshape(count, width, rows)
    imag = spectrum[:, rows:].reshape(count, width, rows)
    ref[:, 0] = real
    if not masked:
        ref[:, 1] = imag
        return
    first = lax.broadcasted_iota(jnp.int32, (count, width, rows), 2) == 0
    ref[:, 1] = jnp.where(first, 0.0, imag)
    ref[:, 2] = jnp.where(first, imag, real)


def emitter(us, width, rows, factor):
    lane = lax.broadcasted_iota(jnp.int32, (width, rows), 1)
    weight = jnp.where(lane == 0, 1.0, 2.0) * (factor / (2 * rows))
    sign = jnp.where(lane < rows // 2, 1.0, -1.0) * weight

    def emit(i, now, before):
        base = pl.multiple_of(i * width, width)
        us[pl.ds(base, width), 0:rows] = now[0] * weight + before[0] * sign
        us[pl.ds(base, width), rows : 2 * rows] = now[1] * weight + before[1] * sign

    return emit


def convolve(xs, ls, us):
    count, _, width, rows = xs.shape
    emit = emitter(us, width, rows, 1.0)
    zero = jnp.zeros((width, rows), f32)
    lane = lax.broadcasted_iota(jnp.int32, (width, rows), 1)

    def outer(i, before):
        def inner(b, total):
            xr, lr, li, lq = xs[i - b, 0], ls[b, 0], ls[b, 1], ls[b, 2]
            xi = jnp.where(lane == 0, xs[i - b, 2], xs[i - b, 1])
            return (total[0] + (xr * lr - xi * li), total[1] + (xr * li + xi * lq))

        now = lax.fori_loop(0, i + 1, inner, (zero, zero))
        emit(i, now, before)
        return now

    lax.fori_loop(0, count, outer, (zero, zero))


def correlate(ref, cs, us, factor):
    count, _, width, rows = ref.shape
    emit = emitter(us, width, rows, factor)
    zero = jnp.zeros((width, rows), f32)

    def outer(n, before):
        d = count - 1 - n

        def inner(b, total):
            cr, ci = cs[b + d, 0], cs[b + d, 1]
            ar, ai, aq = ref[b, 0], ref[b, 1], ref[b, 2]
            return (total[0] + (cr * ar + ci * ai), total[1] + (ci * aq - cr * ai))

        now = lax.fori_loop(0, n + 1, inner, (zero, zero))
        emit(d, now, before)
        return now

    lax.fori_loop(0, count, outer, (zero, zero))


def filters_kernel(in_ref, st_ref, mt_ref, fh_ref, fl_ref, ks, mid, xs, ext, wide, turned):
    tiles = ext.shape[0]
    _, _, width, rows = xs.shape
    table = (fh_ref[...], fl_ref[...])
    short_causal(in_ref[:, :rows].astype(f32).T, 1, ext, st_ref, width, ks, 0)
    short_causal(in_ref[:, rows:].astype(f32).T, 2, ext, st_ref, width, wide, MED + 8)
    put(wide, 8, from_before(get(wide, 8 + rows, MED), width))
    for h in range(tiles):
        wide[h, 0:8, :] = jnp.zeros((8, LANES), f32)
    medium(wide, turned, mt_ref, mid, False)
    keep(xs, halves((get(ks, 0, rows) * get(mid, 0, rows)).T), table, True)


def gates_kernel(scale, in_ref, pos_ref, st_ref, fh_ref, fl_ref, xs, gl_ref, qs, og, cs, ext, us):
    count, _, width, rows = xs.shape
    table = (fh_ref[...], fl_ref[...])
    short_causal(in_ref[:, :rows].astype(f32).T, 0, ext, st_ref, width, qs, 0)
    stretches = pos_ref.shape[0]
    stretch = jnp.concatenate(
        [in_ref[b * width : (b + 1) * width, 4 * rows :] for b in range(count)], 1
    )
    for a in range(count):
        spot = lax.broadcasted_iota(jnp.int32, (stretches, rows), 1) + a * rows
        onehot = (pos_ref[...] == spot).astype(f32).astype(bf16)
        placed = jnp.dot(stretch, onehot, preferred_element_type=f32)
        piece = in_ref[a * width : (a + 1) * width, rows : 2 * rows].astype(f32) + placed
        us[a * width : (a + 1) * width, 0:rows] = piece
    put(og, 0, us[:, 0:rows].T)

    keep(cs, halves((get(og, 0, rows) * get(qs, 0, rows)).T), table, False)
    correlate(xs, cs, us, scale)
    high, low = halves(product(halves(us[...]), table, ((1,), (1,))))
    gl_ref[:, :rows] = high
    gl_ref[:, rows:] = low


def output_kernel(l_ref, xs, qs, og, st_ref, fh_ref, fl_ref, out_ref, ls, ext, us):
    _, _, width, rows = xs.shape
    table = (fh_ref[...], fl_ref[...])
    keep(ls, (l_ref[:, 2 * rows : 3 * rows], l_ref[:, 3 * rows : 4 * rows]), table, True)
    convolve(xs, ls, us)
    long_out = product(table, halves(us[...]), ((1,), (1,)))
    out_ref[:, 0:rows] = (get(qs, 0, rows) * long_out).T.astype(bf16)
    short_anti(get(og, 0, rows) * long_out, 0, ext, st_ref, width, out_ref, 1)


def back_kernel(ls, cs, ks, mid, st_ref, mt_ref, fh_ref, fl_ref, out_ref, ext, wide, turned, us, vb):
    _, _, width, rows = ls.shape
    table = (fh_ref[...], fl_ref[...])
    correlate(ls, cs, us, 1.0)
    inner_grad = product(table, halves(us[...]), ((1,), (1,)))
    mid_back = inner_grad * get(ks, 0, rows)
    put(wide, 0, mid_back)
    put(wide, rows, from_after(mid_back[:MED], width))
    for h in range(ext.shape[0]):
        wide[h, rows + MED : rows + MED + 8, :] = jnp.zeros((8, LANES), f32)
    short_anti(inner_grad * get(mid, 0, rows), 1, ext, st_ref, width, out_ref, 0)
    medium(wide, turned, mt_ref, vb, True)
    short_anti(get(vb, 0, rows), 2, ext, st_ref, width, out_ref, 1)


def whole_spec(n):
    return [pl.BlockSpec(memory_space=pltpu.VMEM)] * n


def local(
    q_proj, k_proj, v_proj, short_taps, medium_taps, long_taps, grad_out, stretch_grads, positions
):
    rows, lanes = q_proj.shape
    count = lax.axis_size("seq")
    index = lax.axis_index("seq")
    width = lanes // count
    tiles = lanes // LANES

    shape = jax.ShapeDtypeStruct

    def call(kernel, outs, args, scratch=(), micros=3):
        many = len(outs) > 1
        return pl.pallas_call(
            kernel,
            out_shape=outs if many else outs[0],
            in_specs=whole_spec(len(args)),
            out_specs=whole_spec(len(outs)) if many else whole_spec(1)[0],
            scratch_shapes=list(scratch),
            cost_estimate=pl.CostEstimate(
                flops=micros * 10**9, bytes_accessed=micros * 3 * 10**6, transcendentals=0
            ),
        )(*args)

    def regroup(array):
        split = array.reshape(count, width, array.shape[1])
        moved = lax.all_to_all(split, "seq", split_axis=0, concat_axis=0, tiled=True)
        return moved.reshape(array.shape)

    pair = shape((lanes, 2 * rows), bf16)
    signal = shape((tiles, rows, LANES), f32)
    three = shape((count, 3, width, rows), f32)
    two = shape((count, 2, width, rows), f32)
    ext = pltpu.VMEM((tiles, rows + 8, LANES), f32)
    wide = pltpu.VMEM((tiles, rows + MED + 8, LANES), f32)
    turned = pltpu.VMEM((8, tiles, rows + MED, LANES), f32)
    spectrum = pltpu.VMEM((lanes, 2 * rows), f32)

    first_packed = call(pack_first_kernel, [pair], (k_proj, v_proj))
    first_arrived = regroup(first_packed)
    members = lax.axis_size("chan")
    stretches = stretch_grads.shape[0]
    packed = pl.pallas_call(
        pack_kernel,
        out_shape=shape((lanes, 4 * rows + members * stretches), bf16),
        in_specs=whole_spec(4),
        out_specs=whole_spec(1)[0],
        scratch_shapes=[
            pltpu.VMEM((members, stretches, lanes), bf16),
            pltpu.SemaphoreType.DMA((members,)),
            pltpu.SemaphoreType.DMA((members,)),
            pltpu.SemaphoreType.DMA,
        ],
        compiler_params=pltpu.CompilerParams(
            collective_id=0 if members > 1 else None, has_side_effects=True
        ),
        name="pack",
    )(q_proj, grad_out, long_taps, stretch_grads)
    arrived = regroup(packed)

    def spread(taps):
        part = lax.dynamic_slice_in_dim(taps, index * width, width, 1)
        part = jnp.tile(part, (1, count))
        return part.reshape(taps.shape[0], tiles, LANES).transpose(1, 0, 2)

    short = spread(jnp.pad(short_taps, ((0, 0), (0, 1), (0, 0))).reshape(24, lanes))
    medium_part = spread(medium_taps)
    fh, fl = halves(fourier(rows))
    ks, mid, xs = call(
        filters_kernel,
        [signal, signal, three],
        (first_arrived, short, medium_part, fh, fl),
        (ext, wide, turned),
        10,
    )
    gl, qs, og, cs = call(
        functools.partial(gates_kernel, (rows * count) ** (-0.5)),
        [pair, signal, signal, two],
        (arrived, positions[:, None], short, fh, fl, xs),
        (ext, spectrum),
        10,
    )
    gl_back = regroup(gl)
    y_gq, ls = call(
        output_kernel, [pair, three], (arrived, xs, qs, og, short, fh, fl), (ext, spectrum), 8
    )
    y_back = regroup(y_gq)
    gk_gv = call(
        back_kernel,
        [pair],
        (ls, cs, ks, mid, short, medium_part, fh, fl),
        (ext, wide, turned, spectrum, pltpu.VMEM((tiles, rows, LANES), f32)),
        12,
    )
    k_back = regroup(gk_gv)
    half = shape((rows, lanes), bf16)
    grad_long = call(unpack_long_kernel, [shape((rows, lanes), f32)], (gl_back,))
    y_out, grad_q = call(unpack_kernel, [half, half], (y_back,))
    grad_k, grad_v = call(unpack_kernel, [half, half], (k_back,))
    return (y_out, grad_q, grad_k, grad_v, grad_long)


def solution(mesh):
    return jax.shard_map(
        local,
        mesh=mesh,
        in_specs=(
            P("seq", "chan"),
            P("seq", "chan"),
            P("seq", "chan"),
            P(None, None, "chan"),
            P(None, "chan"),
            P("seq", "chan"),
            P("seq", "chan"),
            P(("seq", "chan"), None),
            P(),
        ),
        out_specs=(
            P("seq", "chan"),
            P("seq", "chan"),
            P("seq", "chan"),
            P("seq", "chan"),
            P("seq", "chan"),
        ),
        check_vma=False,
    )
```
